512 devices in a mesh: subj: 16 (over y, z_hi), vox: 32 (over z_lo, x, core).
Axes of the slice: x: 4, y: 4, z: 16 (z_hi: 4, z_lo: 4; z = z_hi * 4 + z_lo), core: 2. Of those that a mesh axis runs over, the one named last changes fastest.
Arguments:
- contrasts: bfloat16 [1792, 64, 9919], P('subj', 'vox'), may hold values from -60 to 60
- flips: int32 [48, 1792], P(None, 'subj'), may hold values from -1 to 1, as said below
- mask: int32 [64, 9919], P('vox'), may hold values 0 or 1
Outputs:
- highest: float32 [64, 9919], P('vox')
- exceed: float32 [64, 9919], P('vox')
The draws below stay inside these ranges and needn't reach their ends.
Inputs may be any that keep to these rules, and one draw needn't show every extreme that they name: `flips`: every entry is -1 or +1.
All inputs are finite; a program needn't handle non-finite values. No bound on the sum of `mask` on one device may be relied on, other than what follows from the above.
Results may differ from the reference program's by a relative error of at most 0.0003.
Values sent between devices are 32-bit elements; how exact they have to be, the bound alone decides.
A program may use at most 64 MiB of HBM per device.

```python
import math
import jax
import jax.numpy as jnp
from jax import lax

S_DEV = 112
PY = 109
RADIUS = 2
FB = 16
NB = 3
NF = 48
PLANE = 9919
SUBJ = 1792
NZ = 64
N_SUBJ = 16


def draw_contrasts(key, part):
    keys = jax.random.split(key, 4)
    voxel_scale = jnp.exp(jax.random.uniform(keys[0], (NZ, PLANE), jnp.float32, jnp.log(0.3), jnp.log(3.0)))
    subject_scale = jnp.exp(jax.random.uniform(keys[1], (SUBJ, 1, 1), jnp.float32, jnp.log(0.5), jnp.log(2.0)))
    spread_factor = 1.0 / SUBJ ** 0.5
    effect = jax.random.uniform(keys[2], (NZ, PLANE), jnp.float32, -3.0, 3.0) * spread_factor
    noise = jnp.clip(jax.random.normal(keys[3], (SUBJ, NZ, PLANE), jnp.float32), -5.0, 5.0)
    values = (effect[None] + noise * subject_scale) * voxel_scale[None]
    return values.astype(jnp.bfloat16)


def draw_flips(key, part):
    bits = jax.random.randint(jax.random.fold_in(key, 7), (NF, SUBJ), 0, 2, jnp.int32)
    return 2 * bits - 1


def touch_ends(values, key, least, high):
    place = [jax.random.randint(jax.random.fold_in(key, axis), (), 0, length) for axis, length in enumerate(values.shape)]
    main_axis = values.shape.index(max(values.shape))
    next_to = place[:main_axis] + [(place[main_axis] + 1) % values.shape[main_axis]] + place[main_axis + 1:]
    return values.at[tuple(place)].set(least).at[tuple(next_to)].set(high)


def setup_inputs(seed: int = 0) -> dict:
    seeds = jax.random.split(jax.random.key(seed), 4)
    return {
        "contrasts": draw_contrasts(jax.random.fold_in(seeds[3], 71), 0),
        "flips": draw_flips(jax.random.fold_in(seeds[3], 71), 0),
        "mask": touch_ends((jax.random.randint(seeds[2], (NZ, PLANE), 0, 4) < 3).astype(jnp.int32), jax.random.fold_in(seeds[2], 1), 0, 1),
    }


epsilon = 1e-06

def along_plane(volume, stride):
    margin = RADIUS * stride
    widths = [(0, 0)] * (volume.ndim - 1) + [(margin, margin)]
    padded = jnp.pad(volume, widths)
    length = volume.shape[-1]
    column = jnp.arange(length) % PY
    result = jnp.zeros(volume.shape, jnp.float32)
    for offset in range(-RADIUS, RADIUS + 1):
        begin = margin + offset * stride
        shifted = padded[..., begin:begin + length]
        if stride == 1:
            inside = (column + offset >= 0) & (column + offset < PY)
            shifted = jnp.where(inside, shifted, jnp.zeros_like(shifted))
        result = result + math.exp(-0.5 * offset * offset) * shifted
    return result

def along_depth(padded, depth):
    result = jnp.zeros((padded.shape[0], depth, padded.shape[2]), jnp.float32)
    for offset in range(-RADIUS, RADIUS + 1):
        result = result + math.exp(-0.5 * offset * offset) * padded[:, RADIUS + offset:RADIUS + offset + depth]
    return result

def depth_weights(positions, total):
    result = jnp.zeros(positions.shape, jnp.float32)
    for offset in range(-RADIUS, RADIUS + 1):
        inside = ((positions + offset >= 0) & (positions + offset < total)).astype(jnp.float32)
        result = result + math.exp(-0.5 * offset * offset) * inside
    return result

def smooth(volume):
    flat = along_plane(along_plane(volume, 1), PY)
    padded = jnp.pad(flat, ((0, 0), (RADIUS, RADIUS), (0, 0)))
    summed = along_depth(padded, NZ)
    plane_norm = along_plane(along_plane(jnp.ones((PLANE,), jnp.float32), 1), PY)
    depth_norm = depth_weights(jnp.arange(NZ, dtype=jnp.int32), NZ)
    return summed / (plane_norm[None, None, :] * depth_norm[None, :, None])

def reference(contrasts, flips, mask):
    values = contrasts.reshape(SUBJ, NZ * PLANE)
    totals = jnp.zeros((NF, NZ * PLANE), jnp.float32)
    linear = jnp.zeros((NZ * PLANE,), jnp.float32)
    second = jnp.zeros((NZ * PLANE,), jnp.float32)
    for block_index in range(N_SUBJ):
        block = values[block_index * S_DEV:(block_index + 1) * S_DEV].astype(jnp.float32)
        sign_rows = flips[:, block_index * S_DEV:(block_index + 1) * S_DEV].astype(jnp.float32)
        totals = totals + jnp.dot(sign_rows, block, precision=lax.Precision.HIGHEST)
        linear = linear + lax.optimization_barrier(jnp.sum(block, axis=0))
        second = second + lax.optimization_barrier(jnp.sum(block * block, axis=0))
    number = jnp.float32(SUBJ)
    second = second.reshape(1, NZ, PLANE)
    sigma = jnp.sqrt(smooth(second / number) + epsilon)[0]
    denominator = jnp.sqrt(number) * sigma
    observed = linear.reshape(NZ, PLANE) / denominator
    highest = jnp.full((NZ, PLANE), -1e+30, jnp.float32)
    exceed = jnp.zeros((NZ, PLANE), jnp.float32)
    for batch_index in range(NB):
        block_sums = totals[batch_index * FB:(batch_index + 1) * FB].reshape(FB, NZ, PLANE)
        tflip = block_sums / denominator[None]
        highest = jnp.maximum(highest, lax.optimization_barrier(jnp.max(tflip, axis=0)))
        exceed = exceed + lax.optimization_barrier(jnp.sum(jax.nn.sigmoid(2.0 * (tflip - observed[None])), axis=0))
    inside = mask.astype(jnp.float32)
    return (highest * inside, exceed / NF * inside)
```

```python
import functools
import math

import jax
import jax.numpy as jnp
from jax import lax
from jax.experimental import pallas as pl
from jax.experimental.pallas import tpu as pltpu
from jax.sharding import PartitionSpec as P

NX = 91
PY = 109
PLANE = NX * PY
NZ = 64
NF = 48
SUBJ = 1792
RADIUS = 2
EPSILON = 1e-06

LANES = 640
PIECES = 16
WIDE = LANES * PIECES
PAIR = 2 * LANES
BLOCK = 256
GROUP = 8
CHUNKS = NF // GROUP
EXTRA = CHUNKS
MARGIN = 256
ORDER = (0, 1, 2, EXTRA, 3, 4, 5)

WEIGHT = {k: math.exp(-0.5 * k * k) for k in range(-RADIUS, RADIUS + 1)}
MESH = pl.DeviceIdType.MESH


def row_of(position):
    return (position * 38480) >> 22


def first_bit(i):
    return ((i + 1) // 2) % 2


def second_bit(i):
    return i // 2


def partner(i, kind):
    odd = i % 2
    return (i + 1 - 2 * odd) if kind == 0 else (i + 3 + 2 * odd) % 4


def kernel(
    x_hbm, flips_ref, high_ref, exceed_ref,
    x, w, full, extra, r1, r2, r3, r4, e1, e2, e3, e4, s2, s3, s4, t2, t3, t4,
    square, swept, smooth, before, after, gathered,
    in_sem, send_sem, recv_sem, halo_send, halo_recv, gather_send, gather_recv,
):
    subj = lax.axis_index("subj")
    vox = lax.axis_index("vox")
    n_vox = lax.axis_size("vox")
    y, z = subj // 4, subj % 4
    up = (vox + 1) % n_vox
    down = (vox + n_vox - 1) % n_vox

    def y_peer(kind):
        return {"subj": partner(y, kind) * 4 + z}

    def z_peer(kind):
        return {"subj": y * 4 + partner(z, kind)}

    loads = []
    for j in range(8):
        stop = min(PAIR * (j + 1), PLANE)
        view = (slice(None), slice(None), pl.ds(PAIR * j, stop - PAIR * j))
        load = pltpu.make_async_copy(x_hbm.at[view], x.at[view], in_sem.at[j])
        load.start()
        loads.append(load)

    barrier = pltpu.get_barrier_semaphore()
    for kind in range(2):
        pl.semaphore_signal(barrier, 1, device_id=y_peer(kind), device_id_type=MESH)
        pl.semaphore_signal(barrier, 1, device_id=z_peer(kind), device_id_type=MESH)
    for other in (up, down):
        pl.semaphore_signal(barrier, 1, device_id={"vox": other}, device_id_type=MESH)

    signs = flips_ref[...].astype(jnp.float32).astype(jnp.bfloat16)
    n_local = signs.shape[1]
    column = lax.broadcasted_iota(jnp.int32, (n_local, 2 * n_local), 1)
    subject = lax.broadcasted_iota(jnp.int32, (n_local, 2 * n_local), 0)
    for p in range(2):
        spread = (column == 2 * subject + p).astype(jnp.float32).astype(jnp.bfloat16)
        w[pl.ds(NF * p, NF), :] = jnp.dot(
            signs, spread, preferred_element_type=jnp.float32
        ).astype(jnp.bfloat16)
    lane = lax.broadcasted_iota(jnp.int32, (16, 2 * n_local), 1)
    line = lax.broadcasted_iota(jnp.int32, (16, 2 * n_local), 0)
    w[pl.ds(2 * NF, 16), :] = (lane % 2 == line).astype(jnp.float32).astype(jnp.bfloat16)

    square[:, pl.ds(0, MARGIN)] = jnp.zeros((2, MARGIN), jnp.float32)
    square[:, pl.ds(MARGIN + WIDE - LANES, LANES + MARGIN)] = jnp.zeros((2, LANES + MARGIN), jnp.float32)
    swept[:, pl.ds(0, MARGIN)] = jnp.zeros((2, MARGIN), jnp.float32)
    swept[:, pl.ds(MARGIN + WIDE, MARGIN)] = jnp.zeros((2, MARGIN), jnp.float32)
    for p in range(2):
        for g in range(CHUNKS):
            full[p, g, PIECES - 1] = jnp.zeros((GROUP, LANES), jnp.float32)
        extra[p, PIECES - 1] = jnp.zeros((2, LANES), jnp.float32)

    def block(start, width, piece_of):
        values = x[:, :, pl.ds(start, width)].reshape(2 * n_local, width)
        sums = jnp.dot(w[...], values, preferred_element_type=jnp.float32)
        wide = values.astype(jnp.float32)
        squared = jnp.sum((wide * wide).reshape(n_local // 4, 8, width), axis=0)
        second = squared[0:2] + squared[2:4] + squared[4:6] + squared[6:8]
        square[:, pl.ds(MARGIN + start, width)] = second
        for part in range(2):
            low = 128 * part
            size = min(128, width - low)
            piece, offset = piece_of(part)
            place = pl.ds(offset, size)
            for p in range(2):
                for g in range(CHUNKS):
                    row = NF * p + GROUP * g
                    full[p, g, piece, :, place] = sums[row:row + GROUP, low:low + size]
                row = 2 * NF + p
                extra[p, piece, pl.ds(0, 1), place] = sums[row:row + 1, low:low + size]

    def pair(j, count, last_width):
        base = pl.multiple_of(j * PAIR, 128) if not isinstance(j, int) else j * PAIR
        for i in range(count):
            def piece_of(part, i=i):
                tile = 2 * i + part
                return 2 * j + tile // 5, 128 * (tile % 5)
            block(base + BLOCK * i, last_width if i == count - 1 else BLOCK, piece_of)

    for j in range(7):
        loads[j].wait()

    @pl.loop(0, 7)
    def _(j):
        pair(j, 5, BLOCK)

    loads[7].wait()
    rest = PLANE - 7 * PAIR
    pair(7, pl.cdiv(rest, BLOCK), rest - BLOCK * (pl.cdiv(rest, BLOCK) - 1))

    pl.semaphore_wait(barrier, 6)

    keep = []
    for p in range(2):
        bits = (first_bit, second_bit) if p == 0 else (second_bit, first_bit)
        keep.append([bits[0](y), bits[1](y), bits[0](z), bits[1](z)])

    def send_of(step, p, c):
        k1 = keep[p][0]
        if c == EXTRA:
            source = [extra.at[p, pl.ds(8 * (1 - k1), 8)], t2.at[p], t3.at[p], t4.at[p]][step]
            target = [e1, e2, e3, e4][step].at[p]
        else:
            source = [full.at[p, c, pl.ds(8 * (1 - k1), 8)], s2.at[p, c], s3.at[p, c], s4.at[p, c]][step]
            target = [r1, r2, r3, r4][step].at[p, c]
        peer = [y_peer(p), y_peer(1 - p), z_peer(p), z_peer(1 - p)][step]
        return pltpu.make_async_remote_copy(
            src_ref=source, dst_ref=target,
            send_sem=send_sem.at[step, p, c], recv_sem=recv_sem.at[step, p, c],
            device_id=peer, device_id_type=MESH,
        )

    def views(p, c):
        if c == EXTRA:
            return extra.at[p], e1.at[p], e2.at[p], e3.at[p], e4.at[p]
        return full.at[p, c], r1.at[p, c], r2.at[p, c], r3.at[p, c], r4.at[p, c]

    started = []

    def start(step, c):
        for p in range(2):
            copy = send_of(step, p, c)
            copy.start()
            started.append(copy)

    def advance(step, c):
        for p in range(2):
            k1, k2, k3, k4 = keep[p]
            send_of(step, p, c).wait_recv()
            a, b1, b2, b3, _ = views(p, c)
            if step == 0:
                out = t2.at[p] if c == EXTRA else s2.at[p, c]
                for i in range(4):
                    at = 4 * (1 - k2) + i
                    out[i] = a[8 * k1 + at] + b1[at]
            elif step == 1:
                out = t3.at[p] if c == EXTRA else s3.at[p, c]
                for i in range(2):
                    at = 2 * (1 - k3) + i
                    out[i] = a[8 * k1 + 4 * k2 + at] + b1[4 * k2 + at] + b2[at]
            elif step == 2:
                out = t4.at[p] if c == EXTRA else s4.at[p, c]
                at = 1 - k4
                out[0] = a[8 * k1 + 4 * k2 + 2 * k3 + at] + b1[4 * k2 + 2 * k3 + at] + b2[2 * k3 + at] + b3[at]
            copy = send_of(step + 1, p, c)
            copy.start()
            started.append(copy)

    def total(p, c):
        k1, k2, k3, k4 = keep[p]
        a, b1, b2, b3, b4 = views(p, c)
        return a[8 * k1 + 4 * k2 + 2 * k3 + k4] + b1[4 * k2 + 2 * k3 + k4] + b2[2 * k3 + k4] + b3[k4] + b4[0]

    start(0, ORDER[0])
    start(0, ORDER[1])

    SEG = 1280

    def shifted(ref, base, offset):
        padded = ref[:, pl.ds(base, SEG + 2 * MARGIN)]
        return pltpu.roll(padded, (-offset) % (SEG + 2 * MARGIN), 1)[:, MARGIN:MARGIN + SEG]

    @pl.loop(0, WIDE // SEG)
    def _(i):
        base = pl.multiple_of(i * SEG, 128)
        position = base + lax.broadcasted_iota(jnp.int32, (2, SEG), 1)
        at = position - PY * row_of(position)
        result = jnp.zeros((2, SEG), jnp.float32)
        for k in range(-RADIUS, RADIUS + 1):
            moved = shifted(square, base, k)
            inside = (at + k >= 0) & (at + k < PY)
            result = result + WEIGHT[k] * jnp.where(inside, moved, 0.0)
        swept[:, pl.ds(pl.multiple_of(base + MARGIN, 128), SEG)] = result

    @pl.loop(0, WIDE // SEG)
    def _(i):
        base = pl.multiple_of(i * SEG, 128)
        result = jnp.zeros((2, SEG), jnp.float32)
        for k in range(-RADIUS, RADIUS + 1):
            result = result + WEIGHT[k] * shifted(swept, base, k * PY)
        smooth[:, pl.ds(base, SEG)] = result

    halo = [
        pltpu.make_async_remote_copy(
            src_ref=smooth, dst_ref=target, send_sem=halo_send.at[i], recv_sem=halo_recv.at[i],
            device_id={"vox": other}, device_id_type=MESH,
        )
        for i, (target, other) in enumerate(((before, up), (after, down)))
    ]
    for copy in halo:
        copy.start()

    def depth():
        for copy in halo:
            copy.wait_recv()
        first = vox > 0
        last = vox < n_vox - 1
        for i in range(PIECES):
            place = pl.ds(LANES * i, LANES)
            lower = jnp.where(first, before[:, place], 0.0)
            upper = jnp.where(last, after[:, place], 0.0)
            own = smooth[:, place]
            extra[0, i, pl.ds(1, 1), :] = (
                WEIGHT[2] * lower[0:1] + WEIGHT[1] * lower[1:2] + own[0:1] + WEIGHT[1] * own[1:2] + WEIGHT[2] * upper[0:1]
            )
            extra[1, i, pl.ds(1, 1), :] = (
                WEIGHT[2] * lower[1:2] + WEIGHT[1] * own[0:1] + own[1:2] + WEIGHT[1] * upper[0:1] + WEIGHT[2] * upper[1:2]
            )

    n = len(ORDER)
    for t in range(n + 4):
        if t < n:
            advance(0, ORDER[t])
            if t + 2 < n:
                if ORDER[t + 2] == EXTRA:
                    depth()
                start(0, ORDER[t + 2])
        if 0 <= t - 1 < n:
            advance(1, ORDER[t - 1])
        if 0 <= t - 3 < n:
            advance(2, ORDER[t - 3])

    number = jnp.float32(SUBJ)

    def wait_last(c):
        for p in range(2):
            send_of(3, p, c).wait_recv()

    for c in ORDER:
        wait_last(c)

    owned = []
    for p in range(2):
        k1, k2, k3, k4 = keep[p]
        piece = 8 * k1 + 4 * k2 + 2 * k3 + k4
        owned.append(piece)
        position = piece * LANES + lax.broadcasted_iota(jnp.int32, (1, LANES), 1)
        at_x = row_of(position)
        at_y = position - PY * at_x
        level = 2 * vox + p + jnp.zeros((1, LANES), jnp.int32)
        norms = []
        for at, size in ((at_x, NX), (at_y, PY), (level, NZ)):
            norm = jnp.zeros((1, LANES), jnp.float32)
            for k in range(-RADIUS, RADIUS + 1):
                norm = norm + jnp.where((at + k >= 0) & (at + k < size), jnp.float32(WEIGHT[k]), 0.0)
            norms.append(norm)
        sums = total(p, EXTRA)
        sigma = jnp.sqrt(sums[1:2] / number / (norms[0] * norms[1] * norms[2]) + EPSILON)
        denominator = jnp.sqrt(number) * sigma
        observed = sums[0:1] / denominator
        best = jnp.full((GROUP, LANES), -1e30, jnp.float32)
        share = jnp.zeros((GROUP, LANES), jnp.float32)
        for g in range(CHUNKS):
            tflip = total(p, g) / denominator
            best = jnp.maximum(best, tflip)
            share = share + jax.nn.sigmoid(2.0 * (tflip - observed))
        gathered[p, piece, pl.ds(0, 1), :] = jnp.max(best, axis=0, keepdims=True)
        gathered[p, piece, pl.ds(1, 1), :] = jnp.sum(share, axis=0, keepdims=True) / NF

    for step in range(4):
        copies = []
        size = 1 << step
        for p in range(2):
            peer = [z_peer(1 - p), z_peer(p), y_peer(1 - p), y_peer(p)][step]
            place = gathered.at[p, pl.ds(owned[p] // size * size, size)]
            copies.append(pltpu.make_async_remote_copy(
                src_ref=place, dst_ref=place, send_sem=gather_send.at[step, p], recv_sem=gather_recv.at[step, p],
                device_id=peer, device_id_type=MESH,
            ))
        for copy in copies:
            copy.start()
        for copy in copies:
            copy.wait_recv()
        started.extend(copies)

    for i in range(PIECES):
        width = min(LANES, PLANE - LANES * i)
        for p in range(2):
            block_of = gathered[p, i]
            high_ref[pl.ds(p, 1), pl.ds(LANES * i, width)] = block_of[0:1, :width]
            exceed_ref[pl.ds(p, 1), pl.ds(LANES * i, width)] = block_of[1:2, :width]

    for copy in started + halo:
        copy.wait_send()


def per_device(contrasts, flips, mask):
    local, depth, cells = contrasts.shape
    f32 = jnp.float32
    vmem = pltpu.VMEM
    high, exceed = pl.pallas_call(
        kernel,
        out_shape=[jax.ShapeDtypeStruct((depth, cells), f32)] * 2,
        in_specs=[pl.BlockSpec(memory_space=pl.ANY), pl.BlockSpec(memory_space=vmem)],
        out_specs=[pl.BlockSpec(memory_space=vmem)] * 2,
        scratch_shapes=[
            vmem((local, 2, cells), jnp.bfloat16),
            vmem((2 * NF + 16, 2 * local), jnp.bfloat16),
            vmem((2, CHUNKS, PIECES, GROUP, LANES), f32),
            vmem((2, PIECES, 2, LANES), f32),
            *[vmem((2, CHUNKS, m, GROUP, LANES), f32) for m in (8, 4, 2, 1)],
            *[vmem((2, m, 2, LANES), f32) for m in (8, 4, 2, 1)],
            *[vmem((2, CHUNKS, m, GROUP, LANES), f32) for m in (4, 2, 1)],
            *[vmem((2, m, 2, LANES), f32) for m in (4, 2, 1)],
            vmem((2, WIDE + 2 * MARGIN), f32),
            vmem((2, WIDE + 2 * MARGIN), f32),
            vmem((2, WIDE), f32),
            vmem((2, WIDE), f32),
            vmem((2, WIDE), f32),
            vmem((2, PIECES, 2, LANES), f32),
            pltpu.SemaphoreType.DMA((8,)),
            pltpu.SemaphoreType.DMA((4, 2, CHUNKS + 1)),
            pltpu.SemaphoreType.DMA((4, 2, CHUNKS + 1)),
            pltpu.SemaphoreType.DMA((2,)),
            pltpu.SemaphoreType.DMA((2,)),
            pltpu.SemaphoreType.DMA((4, 2)),
            pltpu.SemaphoreType.DMA((4, 2)),
        ],
        compiler_params=pltpu.CompilerParams(
            collective_id=0, has_side_effects=True, vmem_limit_bytes=60 * 1024 * 1024
        ),
    )(contrasts, flips)
    inside = mask.astype(f32)
    return high * inside, exceed * inside


def solution(mesh):
    in_specs = (P("subj", "vox", None), P(None, "subj"), P("vox", None))
    out_specs = (P("vox", None), P("vox", None))
    return jax.shard_map(
        per_device, mesh=mesh, in_specs=in_specs, out_specs=out_specs, check_vma=False
    )
```

```python
import functools
import math

import jax
import jax.numpy as jnp
from jax import lax
from jax.experimental import pallas as pl
from jax.experimental.pallas import tpu as pltpu
from jax.sharding import PartitionSpec as P

NX = 91
PY = 109
PLANE = NX * PY
NZ = 64
NF = 48
SUBJ = 1792
RADIUS = 2
EPSILON = 1e-06

TILE = 128
PIECES = 16
CHUNKS = 5
SPAN = TILE * PIECES
WIDE = SPAN * CHUNKS
LANES = TILE * CHUNKS
HALVES = 2
GROUP = NF // HALVES
ITEMS = CHUNKS * HALVES
EXTRA = ITEMS
BLOCK = 256
MARGIN = 256
SEG = 1280
ORDER = (0, 1, 2, 3, 4, 5, 6, EXTRA, 7, 8, 9)

WEIGHT = {k: math.exp(-0.5 * k * k) for k in range(-RADIUS, RADIUS + 1)}
MESH = pl.DeviceIdType.MESH


def row_of(position):
    return (position * 38480) >> 22


def first_bit(i):
    return ((i + 1) // 2) % 2


def second_bit(i):
    return i // 2


def partner(i, kind):
    odd = i % 2
    return (i + 1 - 2 * odd) if kind == 0 else (i + 3 + 2 * odd) % 4


def piece_of(p, y, z):
    bits = (first_bit, second_bit) if p == 0 else (second_bit, first_bit)
    return 8 * bits[0](y) + 4 * bits[1](y) + 2 * bits[0](z) + bits[1](z)


OWNER = [{piece_of(p, d // 4, d % 4): d for d in range(PIECES)} for p in range(2)]


def kernel(
    x_hbm, flips_ref, high_ref, exceed_ref,
    x, w, full, extra, r1, r2, r3, r4, e1, e2, e3, e4, s2, s3, s4, t2, t3, t4,
    square, swept, smooth, before, after, gathered,
    in_sem, send_sem, recv_sem, halo_send, halo_recv, gather_send, gather_recv,
):
    subj = lax.axis_index("subj")
    vox = lax.axis_index("vox")
    n_vox = lax.axis_size("vox")
    y, z = subj // 4, subj % 4
    up = (vox + 1) % n_vox
    down = (vox + n_vox - 1) % n_vox

    def y_peer(kind):
        return {"subj": partner(y, kind) * 4 + z}

    def z_peer(kind):
        return {"subj": y * 4 + partner(z, kind)}

    loads = []
    for c in range(CHUNKS):
        width = min(SPAN, PLANE - SPAN * c)
        view = (slice(None), slice(None), pl.ds(SPAN * c, width))
        load = pltpu.make_async_copy(x_hbm.at[view], x.at[view], in_sem.at[c])
        load.start()
        loads.append(load)

    barrier = pltpu.get_barrier_semaphore()
    for kind in range(2):
        pl.semaphore_signal(barrier, 1, device_id=y_peer(kind), device_id_type=MESH)
        pl.semaphore_signal(barrier, 1, device_id=z_peer(kind), device_id_type=MESH)
    for other in (up, down):
        pl.semaphore_signal(barrier, 1, device_id={"vox": other}, device_id_type=MESH)

    signs = flips_ref[...].astype(jnp.float32).astype(jnp.bfloat16)
    n_local = signs.shape[1]
    column = lax.broadcasted_iota(jnp.int32, (n_local, 2 * n_local), 1)
    subject = lax.broadcasted_iota(jnp.int32, (n_local, 2 * n_local), 0)
    for p in range(2):
        spread = (column == 2 * subject + p).astype(jnp.float32).astype(jnp.bfloat16)
        w[pl.ds(NF * p, NF), :] = jnp.dot(
            signs, spread, preferred_element_type=jnp.float32
        ).astype(jnp.bfloat16)
    lane = lax.broadcasted_iota(jnp.int32, (16, 2 * n_local), 1)
    line = lax.broadcasted_iota(jnp.int32, (16, 2 * n_local), 0)
    w[pl.ds(2 * NF, 16), :] = (lane % 2 == line).astype(jnp.float32).astype(jnp.bfloat16)

    def multiply(c):
        loads[c].wait()
        for start in range(SPAN * c, min(SPAN * (c + 1), PLANE), BLOCK):
            width = min(BLOCK, PLANE - start)
            values = x[:, :, pl.ds(start, width)].reshape(2 * n_local, width)
            sums = jnp.dot(w[...], values, preferred_element_type=jnp.float32)
            wide = values.astype(jnp.float32)
            squared = jnp.sum((wide * wide).reshape(n_local // 4, 8, width), axis=0)
            second = squared[0:2] + squared[2:4] + squared[4:6] + squared[6:8]
            square[:, pl.ds(MARGIN + start, width)] = second
            for low in range(0, width, TILE):
                size = min(TILE, width - low)
                piece = (start + low) // TILE - PIECES * c
                for p in range(2):
                    for h in range(HALVES):
                        row = NF * p + GROUP * h
                        full[p, c, h, piece, :, pl.ds(0, size)] = sums[row:row + GROUP, low:low + size]
                    row = 2 * NF + p
                    extra[p, piece, pl.ds(0, 1), pl.ds(TILE * c, size)] = sums[row:row + 1, low:low + size]

    keep = []
    for p in range(2):
        bits = (first_bit, second_bit) if p == 0 else (second_bit, first_bit)
        keep.append([bits[0](y), bits[1](y), bits[0](z), bits[1](z)])

    def views(p, item):
        if item == EXTRA:
            return [ref.at[p] for ref in (extra, e1, e2, e3, e4, t2, t3, t4)]
        at = (p, item // HALVES, item % HALVES)
        return [ref.at[at] for ref in (full, r1, r2, r3, r4, s2, s3, s4)]

    def send_of(step, p, item):
        held = views(p, item)
        source = [held[0].at[pl.ds(8 * (1 - keep[p][0]), 8)], held[5], held[6], held[7]][step]
        peer = [y_peer(p), y_peer(1 - p), z_peer(p), z_peer(1 - p)][step]
        return pltpu.make_async_remote_copy(
            src_ref=source, dst_ref=held[1 + step],
            send_sem=send_sem.at[step, p, item], recv_sem=recv_sem.at[step, p, item],
            device_id=peer, device_id_type=MESH,
        )

    started = {}

    def start(step, p, item):
        copy = send_of(step, p, item)
        copy.start()
        started[step, p, item] = copy

    def advance(step, item):
        for p in range(2):
            k1, k2, k3, k4 = keep[p]
            started[step, p, item].wait_recv()
            a, b1, b2, b3, _, o2, o3, o4 = views(p, item)
            if step == 0:
                for i in range(4):
                    at = 4 * (1 - k2) + i
                    o2[i] = a[8 * k1 + at] + b1[at]
            elif step == 1:
                for i in range(2):
                    at = 2 * (1 - k3) + i
                    o3[i] = a[8 * k1 + 4 * k2 + at] + b1[4 * k2 + at] + b2[at]
            else:
                at = 1 - k4
                o4[0] = a[8 * k1 + 4 * k2 + 2 * k3 + at] + b1[4 * k2 + 2 * k3 + at] + b2[2 * k3 + at] + b3[at]
            start(step + 1, p, item)

    def total(p, item):
        k1, k2, k3, k4 = keep[p]
        started[3, p, item].wait_recv()
        a, b1, b2, b3, b4 = views(p, item)[:5]
        return a[8 * k1 + 4 * k2 + 2 * k3 + k4] + b1[4 * k2 + 2 * k3 + k4] + b2[2 * k3 + k4] + b3[k4] + b4[0]

    def shifted(ref, base, offset):
        padded = ref[:, pl.ds(base, SEG + 2 * MARGIN)]
        return pltpu.roll(padded, (-offset) % (SEG + 2 * MARGIN), 1)[:, MARGIN:MARGIN + SEG]

    def in_plane():
        @pl.loop(0, WIDE // SEG)
        def _(i):
            base = pl.multiple_of(i * SEG, TILE)
            position = base + lax.broadcasted_iota(jnp.int32, (2, SEG), 1)
            at = position - PY * row_of(position)
            result = jnp.zeros((2, SEG), jnp.float32)
            for k in range(-RADIUS, RADIUS + 1):
                moved = shifted(square, base, k)
                inside = (at + k >= 0) & (at + k < PY)
                result = result + WEIGHT[k] * jnp.where(inside, moved, 0.0)
            swept[:, pl.ds(pl.multiple_of(base + MARGIN, TILE), SEG)] = result

        @pl.loop(0, WIDE // SEG)
        def _(i):
            base = pl.multiple_of(i * SEG, TILE)
            result = jnp.zeros((2, SEG), jnp.float32)
            for k in range(-RADIUS, RADIUS + 1):
                result = result + WEIGHT[k] * shifted(swept, base, k * PY)
            smooth[:, pl.ds(base, SEG)] = result

    halo = [
        pltpu.make_async_remote_copy(
            src_ref=smooth, dst_ref=target, send_sem=halo_send.at[i], recv_sem=halo_recv.at[i],
            device_id={"vox": other}, device_id_type=MESH,
        )
        for i, (target, other) in enumerate(((before, up), (after, down)))
    ]

    def depth():
        for copy in halo:
            copy.wait_recv()
        first = vox > 0
        last = vox < n_vox - 1
        for i in range(0, WIDE, SEG):
            place = pl.ds(i, SEG)
            lower = jnp.where(first, before[:, place], 0.0)
            upper = jnp.where(last, after[:, place], 0.0)
            own = smooth[:, place]
            rows = (
                WEIGHT[2] * lower[0:1] + WEIGHT[1] * lower[1:2] + own[0:1] + WEIGHT[1] * own[1:2] + WEIGHT[2] * upper[0:1],
                WEIGHT[2] * lower[1:2] + WEIGHT[1] * own[0:1] + own[1:2] + WEIGHT[1] * upper[0:1] + WEIGHT[2] * upper[1:2],
            )
            for low in range(0, SEG, TILE):
                tile = (i + low) // TILE
                for p in range(2):
                    extra[p, tile % PIECES, pl.ds(1, 1), pl.ds(TILE * (tile // PIECES), TILE)] = rows[p][:, low:low + TILE]

    multiply(0)
    pl.semaphore_wait(barrier, 6)
    for item in ORDER[:2]:
        for p in range(2):
            start(0, p, item)

    zeros = jnp.zeros((2, MARGIN), jnp.float32)
    square[:, pl.ds(0, MARGIN)] = zeros
    edge = PLANE // TILE * TILE
    square[:, pl.ds(MARGIN + edge, WIDE + MARGIN - edge)] = jnp.zeros((2, WIDE + MARGIN - edge), jnp.float32)
    swept[:, pl.ds(0, MARGIN)] = zeros
    swept[:, pl.ds(MARGIN + WIDE, MARGIN)] = zeros
    for p in range(2):
        for i in range(edge // TILE % PIECES, PIECES):
            for h in range(HALVES):
                full[p, CHUNKS - 1, h, i] = jnp.zeros((GROUP, TILE), jnp.float32)
            extra[p, i, pl.ds(0, 1), pl.ds(LANES - TILE, TILE)] = jnp.zeros((1, TILE), jnp.float32)
    multiply(1)

    n = len(ORDER)
    for t in range(n + 3):
        if t < n:
            advance(0, ORDER[t])
            if t + 2 < n:
                if ORDER[t + 2] == EXTRA:
                    depth()
                for p in range(2):
                    start(0, p, ORDER[t + 2])
        if 0 <= t - 1 < n:
            advance(1, ORDER[t - 1])
        if 0 <= t - 3 < n:
            advance(2, ORDER[t - 3])
        if t < 3:
            multiply(t + 2)
        elif t == 3:
            in_plane()
            for copy in halo:
                copy.start()

    number = jnp.float32(SUBJ)
    scales = []
    for p in range(2):
        k1, k2, k3, k4 = keep[p]
        piece = 8 * k1 + 4 * k2 + 2 * k3 + k4
        spot = lax.broadcasted_iota(jnp.int32, (1, LANES), 1)
        position = (PIECES * (spot >> 7) + piece) * TILE + (spot & 127)
        at_x = row_of(position)
        at_y = position - PY * at_x
        level = 2 * vox + p + jnp.zeros((1, LANES), jnp.int32)
        norms = []
        for at, size in ((at_x, NX), (at_y, PY), (level, NZ)):
            norm = jnp.zeros((1, LANES), jnp.float32)
            for k in range(-RADIUS, RADIUS + 1):
                norm = norm + jnp.where((at + k >= 0) & (at + k < size), jnp.float32(WEIGHT[k]), 0.0)
            norms.append(norm)
        sums = total(p, EXTRA)
        sigma = jnp.sqrt(sums[1:2] / number / (norms[0] * norms[1] * norms[2]) + EPSILON)
        denominator = jnp.sqrt(number) * sigma
        scales.append((denominator, sums[0:1] / denominator))

    def finish(c):
        place = slice(TILE * c, TILE * (c + 1))
        for p in range(2):
            denominator, observed = (scale[:, place] for scale in scales[p])
            best = jnp.full((GROUP, TILE), -1e30, jnp.float32)
            share = jnp.zeros((GROUP, TILE), jnp.float32)
            for h in range(HALVES):
                tflip = total(p, HALVES * c + h) / denominator
                best = jnp.maximum(best, tflip)
                share = share + jax.nn.sigmoid(2.0 * (tflip - observed))
            gathered[subj, c, pl.ds(2 * p, 1), :] = jnp.max(best, axis=0, keepdims=True)
            gathered[subj, c, pl.ds(2 * p + 1, 1), :] = jnp.sum(share, axis=0, keepdims=True) / NF

    returned = []

    def give(step, part):
        chunks = pl.ds(0, CHUNKS - 1) if part == 0 else pl.ds(CHUNKS - 1, 1)
        copies = []
        for d in range(1, 4):
            if step == 0:
                place = gathered.at[pl.ds(subj, 1), chunks]
                peer = {"subj": y * 4 + (z + d) % 4}
            else:
                place = gathered.at[pl.ds(4 * y, 4), chunks]
                peer = {"subj": (y + d) % 4 * 4 + z}
            copy = pltpu.make_async_remote_copy(
                src_ref=place, dst_ref=place,
                send_sem=gather_send.at[step, part, d - 1], recv_sem=gather_recv.at[step, part, d - 1],
                device_id=peer, device_id_type=MESH,
            )
            copy.start()
            copies.append(copy)
        returned.extend(copies)
        return copies

    def arrived(copies):
        for copy in copies:
            copy.wait_recv()

    def write(chunks):
        for c in chunks:
            for i in range(PIECES):
                begin = SPAN * c + TILE * i
                width = min(TILE, PLANE - begin)
                if width <= 0:
                    continue
                for p in range(2):
                    for kind, ref in enumerate((high_ref, exceed_ref)):
                        ref[pl.ds(p, 1), pl.ds(begin, width)] = gathered[OWNER[p][i], c, pl.ds(2 * p + kind, 1), pl.ds(0, width)]

    for c in range(CHUNKS - 1):
        finish(c)
    z_early = give(0, 0)
    finish(CHUNKS - 1)
    z_late = give(0, 1)
    arrived(z_early)
    y_early = give(1, 0)
    arrived(z_late)
    y_late = give(1, 1)
    arrived(y_early)
    write(range(CHUNKS - 1))
    arrived(y_late)
    write((CHUNKS - 1,))

    for copy in list(started.values()) + halo + returned:
        copy.wait_send()


def per_device(contrasts, flips, mask):
    local, depth, cells = contrasts.shape
    f32 = jnp.float32
    vmem = pltpu.VMEM
    high, exceed = pl.pallas_call(
        kernel,
        out_shape=[jax.ShapeDtypeStruct((depth, cells), f32)] * 2,
        in_specs=[pl.BlockSpec(memory_space=pl.ANY), pl.BlockSpec(memory_space=vmem)],
        out_specs=[pl.BlockSpec(memory_space=vmem)] * 2,
        scratch_shapes=[
            vmem((local, 2, cells), jnp.bfloat16),
            vmem((2 * NF + 16, 2 * local), jnp.bfloat16),
            vmem((2, CHUNKS, HALVES, PIECES, GROUP, TILE), f32),
            vmem((2, PIECES, 2, LANES), f32),
            *[vmem((2, CHUNKS, HALVES, m, GROUP, TILE), f32) for m in (8, 4, 2, 1)],
            *[vmem((2, m, 2, LANES), f32) for m in (8, 4, 2, 1)],
            *[vmem((2, CHUNKS, HALVES, m, GROUP, TILE), f32) for m in (4, 2, 1)],
            *[vmem((2, m, 2, LANES), f32) for m in (4, 2, 1)],
            vmem((2, WIDE + 2 * MARGIN), f32),
            vmem((2, WIDE + 2 * MARGIN), f32),
            vmem((2, WIDE), f32),
            vmem((2, WIDE), f32),
            vmem((2, WIDE), f32),
            vmem((PIECES, CHUNKS, 4, TILE), f32),
            pltpu.SemaphoreType.DMA((CHUNKS,)),
            pltpu.SemaphoreType.DMA((4, 2, ITEMS + 1)),
            pltpu.SemaphoreType.DMA((4, 2, ITEMS + 1)),
            pltpu.SemaphoreType.DMA((2,)),
            pltpu.SemaphoreType.DMA((2,)),
            pltpu.SemaphoreType.DMA((2, 2, 3)),
            pltpu.SemaphoreType.DMA((2, 2, 3)),
        ],
        compiler_params=pltpu.CompilerParams(
            collective_id=0, has_side_effects=True, vmem_limit_bytes=60 * 1024 * 1024
        ),
    )(contrasts, flips)
    inside = mask.astype(f32)
    return high * inside, exceed * inside


def solution(mesh):
    in_specs = (P("subj", "vox", None), P(None, "subj"), P("vox", None))
    out_specs = (P("vox", None), P("vox", None))
    return jax.shard_map(
        per_device, mesh=mesh, in_specs=in_specs, out_specs=out_specs, check_vma=False
    )
```

```python
import functools
import math

import jax
import jax.numpy as jnp
from jax import lax
from jax.experimental import pallas as pl
from jax.experimental.pallas import tpu as pltpu
from jax.sharding import PartitionSpec as P

NX = 91
PY = 109
PLANE = NX * PY
NZ = 64
NF = 48
SUBJ = 1792
RADIUS = 2
EPSILON = 1e-06

TILE = 128
PIECES = 16
CHUNKS = 5
SPAN = TILE * PIECES
WIDE = SPAN * CHUNKS
LANES = TILE * CHUNKS
ROWS = ((24, 24), (24, 24), (24, 24), (24, 24), (24, 24))
PARTS = [(c, sum(rows[:i]), rows[i]) for c, rows in enumerate(ROWS) for i in range(len(rows))]
ITEMS = len(PARTS)
EXTRA = ITEMS
BLOCK = 256
MARGIN = 256
SEG = 1280
AHEAD = 2
NEXT = 1
WORK = 0
LAG = 3
ENTRY = 7
ORDER = (*range(ENTRY), EXTRA, *range(ENTRY, ITEMS))

WEIGHT = {k: math.exp(-0.5 * k * k) for k in range(-RADIUS, RADIUS + 1)}
MESH = pl.DeviceIdType.MESH


def row_of(position):
    return (position * 38480) >> 22


def first_bit(i):
    return ((i + 1) // 2) % 2


def second_bit(i):
    return i // 2


def partner(i, kind):
    odd = i % 2
    return (i + 1 - 2 * odd) if kind == 0 else (i + 3 + 2 * odd) % 4


def piece_of(p, y, z):
    bits = (first_bit, second_bit) if p == 0 else (second_bit, first_bit)
    return 8 * bits[0](y) + 4 * bits[1](y) + 2 * bits[0](z) + bits[1](z)


OWNER = [{piece_of(p, d // 4, d % 4): d for d in range(PIECES)} for p in range(2)]


def kernel(
    x_hbm, flips_ref, high_ref, exceed_ref,
    x, w, full, extra, r1, r2, r3, r4, e1, e2, e3, e4, s2, s3, s4, t2, t3, t4,
    square, swept, smooth, before, after, gathered,
    in_sem, send_sem, recv_sem, halo_send, halo_recv, gather_send, gather_recv,
    flat_send, flat_recv,
):
    subj = lax.axis_index("subj")
    vox = lax.axis_index("vox")
    n_vox = lax.axis_size("vox")
    y, z = subj // 4, subj % 4
    up = (vox + 1) % n_vox
    down = (vox + n_vox - 1) % n_vox

    def y_peer(kind):
        return {"subj": partner(y, kind) * 4 + z}

    def z_peer(kind):
        return {"subj": y * 4 + partner(z, kind)}

    loads = []
    for c in range(CHUNKS):
        width = min(SPAN, PLANE - SPAN * c)
        view = (slice(None), slice(None), pl.ds(SPAN * c, width))
        load = pltpu.make_async_copy(x_hbm.at[view], x.at[view], in_sem.at[c])
        load.start()
        loads.append(load)

    barrier = pltpu.get_barrier_semaphore()
    for kind in range(2):
        pl.semaphore_signal(barrier, 1, device_id=y_peer(kind), device_id_type=MESH)
        pl.semaphore_signal(barrier, 1, device_id=z_peer(kind), device_id_type=MESH)
    for other in (up, down):
        pl.semaphore_signal(barrier, 1, device_id={"vox": other}, device_id_type=MESH)

    signs = flips_ref[...].astype(jnp.float32).astype(jnp.bfloat16)
    n_local = signs.shape[1]
    column = lax.broadcasted_iota(jnp.int32, (n_local, 2 * n_local), 1)
    subject = lax.broadcasted_iota(jnp.int32, (n_local, 2 * n_local), 0)
    for p in range(2):
        spread = (column == 2 * subject + p).astype(jnp.float32).astype(jnp.bfloat16)
        w[pl.ds(NF * p, NF), :] = jnp.dot(
            signs, spread, preferred_element_type=jnp.float32
        ).astype(jnp.bfloat16)
    lane = lax.broadcasted_iota(jnp.int32, (16, 2 * n_local), 1)
    line = lax.broadcasted_iota(jnp.int32, (16, 2 * n_local), 0)
    w[pl.ds(2 * NF, 16), :] = (lane % 2 == line).astype(jnp.float32).astype(jnp.bfloat16)

    def multiply(c):
        loads[c].wait()
        for start in range(SPAN * c, min(SPAN * (c + 1), PLANE), BLOCK):
            width = min(BLOCK, PLANE - start)
            values = x[:, :, pl.ds(start, width)].reshape(2 * n_local, width)
            sums = jnp.dot(w[...], values, preferred_element_type=jnp.float32)
            wide = values.astype(jnp.float32)
            squared = jnp.sum((wide * wide).reshape(n_local // 4, 8, width), axis=0)
            second = squared[0:2] + squared[2:4] + squared[4:6] + squared[6:8]
            square[:, pl.ds(MARGIN + start, width)] = second
            for low in range(0, width, TILE):
                size = min(TILE, width - low)
                piece = (start + low) // TILE - PIECES * c
                for p in range(2):
                    row = NF * p
                    full[p, c, piece, :, pl.ds(0, size)] = sums[row:row + NF, low:low + size]
                    row = 2 * NF + p
                    extra[p, piece, pl.ds(0, 1), pl.ds(TILE * c, size)] = sums[row:row + 1, low:low + size]

    keep = []
    for p in range(2):
        bits = (first_bit, second_bit) if p == 0 else (second_bit, first_bit)
        keep.append([bits[0](y), bits[1](y), bits[0](z), bits[1](z)])

    def views(p, item):
        if item == EXTRA:
            return [ref.at[p] for ref in (extra, e1, e2, e3, e4, t2, t3, t4)]
        c, row, rows = PARTS[item]
        at = (p, c, slice(None), pl.ds(row, rows))
        return [ref.at[at] for ref in (full, r1, r2, r3, r4, s2, s3, s4)]

    def send_of(step, p, item):
        held = views(p, item)
        source = [held[0].at[pl.ds(8 * (1 - keep[p][0]), 8)], held[5], held[6], held[7]][step]
        peer = [y_peer(p), y_peer(1 - p), z_peer(p), z_peer(1 - p)][step]
        return pltpu.make_async_remote_copy(
            src_ref=source, dst_ref=held[1 + step],
            send_sem=send_sem.at[step, p, item], recv_sem=recv_sem.at[step, p, item],
            device_id=peer, device_id_type=MESH,
        )

    started = {}

    def start(step, p, item):
        copy = send_of(step, p, item)
        copy.start()
        started[step, p, item] = copy

    def advance(step, item):
        for p in range(2):
            k1, k2, k3, k4 = keep[p]
            started[step, p, item].wait_recv()
            a, b1, b2, b3, _, o2, o3, o4 = views(p, item)
            if step == 0:
                for i in range(4):
                    at = 4 * (1 - k2) + i
                    o2[i] = a[8 * k1 + at] + b1[at]
            elif step == 1:
                for i in range(2):
                    at = 2 * (1 - k3) + i
                    o3[i] = a[8 * k1 + 4 * k2 + at] + b1[4 * k2 + at] + b2[at]
            else:
                at = 1 - k4
                o4[0] = a[8 * k1 + 4 * k2 + 2 * k3 + at] + b1[4 * k2 + 2 * k3 + at] + b2[2 * k3 + at] + b3[at]
            start(step + 1, p, item)

    def total(p, item):
        k1, k2, k3, k4 = keep[p]
        started[3, p, item].wait_recv()
        a, b1, b2, b3, b4 = views(p, item)[:5]
        return a[8 * k1 + 4 * k2 + 2 * k3 + k4] + b1[4 * k2 + 2 * k3 + k4] + b2[2 * k3 + k4] + b3[k4] + b4[0]

    def shifted(ref, base, offset):
        padded = ref[:, pl.ds(base, SEG + 2 * MARGIN)]
        return pltpu.roll(padded, (-offset) % (SEG + 2 * MARGIN), 1)[:, MARGIN:MARGIN + SEG]

    def in_plane():
        @pl.loop(0, WIDE // SEG)
        def _(i):
            base = pl.multiple_of(i * SEG, TILE)
            position = base + lax.broadcasted_iota(jnp.int32, (2, SEG), 1)
            at = position - PY * row_of(position)
            result = jnp.zeros((2, SEG), jnp.float32)
            for k in range(-RADIUS, RADIUS + 1):
                moved = shifted(square, base, k)
                inside = (at + k >= 0) & (at + k < PY)
                result = result + WEIGHT[k] * jnp.where(inside, moved, 0.0)
            swept[:, pl.ds(pl.multiple_of(base + MARGIN, TILE), SEG)] = result

        @pl.loop(0, WIDE // SEG)
        def _(i):
            base = pl.multiple_of(i * SEG, TILE)
            result = jnp.zeros((2, SEG), jnp.float32)
            for k in range(-RADIUS, RADIUS + 1):
                result = result + WEIGHT[k] * shifted(swept, base, k * PY)
            smooth[:, pl.ds(base, SEG)] = result

    halo = [
        pltpu.make_async_remote_copy(
            src_ref=smooth, dst_ref=target, send_sem=halo_send.at[i], recv_sem=halo_recv.at[i],
            device_id={"vox": other}, device_id_type=MESH,
        )
        for i, (target, other) in enumerate(((before, up), (after, down)))
    ]

    def depth():
        for copy in halo:
            copy.wait_recv()
        first = vox > 0
        last = vox < n_vox - 1
        for i in range(0, WIDE, SEG):
            place = pl.ds(i, SEG)
            lower = jnp.where(first, before[:, place], 0.0)
            upper = jnp.where(last, after[:, place], 0.0)
            own = smooth[:, place]
            rows = (
                WEIGHT[2] * lower[0:1] + WEIGHT[1] * lower[1:2] + own[0:1] + WEIGHT[1] * own[1:2] + WEIGHT[2] * upper[0:1],
                WEIGHT[2] * lower[1:2] + WEIGHT[1] * own[0:1] + own[1:2] + WEIGHT[1] * upper[0:1] + WEIGHT[2] * upper[1:2],
            )
            for low in range(0, SEG, TILE):
                tile = (i + low) // TILE
                for p in range(2):
                    extra[p, tile % PIECES, pl.ds(1, 1), pl.ds(TILE * (tile // PIECES), TILE)] = rows[p][:, low:low + TILE]

    multiply(0)
    pl.semaphore_wait(barrier, 6)
    for item in ORDER[:AHEAD]:
        for p in range(2):
            start(0, p, item)

    zeros = jnp.zeros((2, MARGIN), jnp.float32)
    square[:, pl.ds(0, MARGIN)] = zeros
    edge = PLANE // TILE * TILE
    square[:, pl.ds(MARGIN + edge, WIDE + MARGIN - edge)] = jnp.zeros((2, WIDE + MARGIN - edge), jnp.float32)
    swept[:, pl.ds(0, MARGIN)] = zeros
    swept[:, pl.ds(MARGIN + WIDE, MARGIN)] = zeros
    for p in range(2):
        for i in range(edge // TILE % PIECES, PIECES):
            full[p, CHUNKS - 1, i] = jnp.zeros((NF, TILE), jnp.float32)
            extra[p, i, pl.ds(0, 1), pl.ds(LANES - TILE, TILE)] = jnp.zeros((1, TILE), jnp.float32)
    multiply(1)

    n = len(ORDER)
    for t in range(n + LAG):
        if t < n:
            advance(0, ORDER[t])
            if t + AHEAD < n:
                if ORDER[t + AHEAD] == EXTRA:
                    depth()
                for p in range(2):
                    start(0, p, ORDER[t + AHEAD])
        if 0 <= t - NEXT < n:
            advance(1, ORDER[t - NEXT])
        if 0 <= t - LAG < n:
            advance(2, ORDER[t - LAG])
        if WORK <= t < WORK + 3:
            multiply(t - WORK + 2)
        elif t == WORK + 3:
            in_plane()
            for copy in halo:
                copy.start()

    number = jnp.float32(SUBJ)
    scales = []
    for p in range(2):
        k1, k2, k3, k4 = keep[p]
        piece = 8 * k1 + 4 * k2 + 2 * k3 + k4
        spot = lax.broadcasted_iota(jnp.int32, (1, LANES), 1)
        position = (PIECES * (spot >> 7) + piece) * TILE + (spot & 127)
        at_x = row_of(position)
        at_y = position - PY * at_x
        level = 2 * vox + p + jnp.zeros((1, LANES), jnp.int32)
        norms = []
        for at, size in ((at_x, NX), (at_y, PY), (level, NZ)):
            norm = jnp.zeros((1, LANES), jnp.float32)
            for k in range(-RADIUS, RADIUS + 1):
                norm = norm + jnp.where((at + k >= 0) & (at + k < size), jnp.float32(WEIGHT[k]), 0.0)
            norms.append(norm)
        sums = total(p, EXTRA)
        sigma = jnp.sqrt(sums[1:2] / number / (norms[0] * norms[1] * norms[2]) + EPSILON)
        denominator = jnp.sqrt(number) * sigma
        scales.append((denominator, sums[0:1] / denominator))

    def finish(c):
        place = slice(TILE * c, TILE * (c + 1))
        for p in range(2):
            denominator, observed = (scale[:, place] for scale in scales[p])
            best = jnp.full((8, TILE), -1e30, jnp.float32)
            share = jnp.zeros((8, TILE), jnp.float32)
            for item, part in enumerate(PARTS):
                if part[0] == c:
                    tflip = total(p, item) / denominator
                    chance = jax.nn.sigmoid(2.0 * (tflip - observed))
                    for low in range(0, part[2], 8):
                        best = jnp.maximum(best, tflip[low:low + 8])
                        share = share + chance[low:low + 8]
            gathered[subj, c, pl.ds(2 * p, 1), :] = jnp.max(best, axis=0, keepdims=True)
            gathered[subj, c, pl.ds(2 * p + 1, 1), :] = jnp.sum(share, axis=0, keepdims=True) / NF

    returned = []

    def give(place, peers, send, recv):
        copies = []
        for d, peer in peers:
            copy = pltpu.make_async_remote_copy(
                src_ref=place, dst_ref=place, send_sem=send.at[d - 1], recv_sem=recv.at[d - 1],
                device_id={"subj": peer}, device_id_type=MESH,
            )
            copy.start()
            copies.append(copy)
        returned.extend(copies)
        return copies

    z_peers = [(d, y * 4 + (z + d) % 4) for d in (2, 1, 3)]
    y_peers = [(d, (y + d) % 4 * 4 + z) for d in (2, 1, 3)]
    early, late = pl.ds(0, CHUNKS - 1), pl.ds(CHUNKS - 1, 1)

    def arrived(copies):
        for copy in copies:
            copy.wait_recv()

    def write(chunks):
        for c in chunks:
            for i in range(PIECES):
                begin = SPAN * c + TILE * i
                width = min(TILE, PLANE - begin)
                if width <= 0:
                    continue
                for p in range(2):
                    for kind, ref in enumerate((high_ref, exceed_ref)):
                        ref[pl.ds(p, 1), pl.ds(begin, width)] = gathered[OWNER[p][i], c, pl.ds(2 * p + kind, 1), pl.ds(0, width)]

    for c in range(CHUNKS - 1):
        finish(c)
    z_early = give(gathered.at[pl.ds(subj, 1), early], z_peers, gather_send.at[0], gather_recv.at[0])
    finish(CHUNKS - 1)
    all_peers = [
        (4 * e + d, (y + e) % 4 * 4 + (z + d) % 4) for d in (2, 1, 3, 0) for e in (2, 1, 3, 0) if d or e
    ]
    flat = give(gathered.at[pl.ds(subj, 1), late], all_peers, flat_send, flat_recv)
    arrived(z_early)
    y_early = give(gathered.at[pl.ds(4 * y, 4), early], y_peers, gather_send.at[1], gather_recv.at[1])
    arrived(y_early)
    write(range(CHUNKS - 1))
    arrived(flat)
    write((CHUNKS - 1,))

    for copy in list(started.values()) + halo + returned:
        copy.wait_send()


def per_device(contrasts, flips, mask):
    local, depth, cells = contrasts.shape
    f32 = jnp.float32
    vmem = pltpu.VMEM
    high, exceed = pl.pallas_call(
        kernel,
        out_shape=[jax.ShapeDtypeStruct((depth, cells), f32)] * 2,
        in_specs=[pl.BlockSpec(memory_space=pl.ANY), pl.BlockSpec(memory_space=vmem)],
        out_specs=[pl.BlockSpec(memory_space=vmem)] * 2,
        scratch_shapes=[
            vmem((local, 2, cells), jnp.bfloat16),
            vmem((2 * NF + 16, 2 * local), jnp.bfloat16),
            vmem((2, CHUNKS, PIECES, NF, TILE), f32),
            vmem((2, PIECES, 2, LANES), f32),
            *[vmem((2, CHUNKS, m, NF, TILE), f32) for m in (8, 4, 2, 1)],
            *[vmem((2, m, 2, LANES), f32) for m in (8, 4, 2, 1)],
            *[vmem((2, CHUNKS, m, NF, TILE), f32) for m in (4, 2, 1)],
            *[vmem((2, m, 2, LANES), f32) for m in (4, 2, 1)],
            vmem((2, WIDE + 2 * MARGIN), f32),
            vmem((2, WIDE + 2 * MARGIN), f32),
            vmem((2, WIDE), f32),
            vmem((2, WIDE), f32),
            vmem((2, WIDE), f32),
            vmem((PIECES, CHUNKS, 4, TILE), f32),
            pltpu.SemaphoreType.DMA((CHUNKS,)),
            pltpu.SemaphoreType.DMA((4, 2, ITEMS + 1)),
            pltpu.SemaphoreType.DMA((4, 2, ITEMS + 1)),
            pltpu.SemaphoreType.DMA((2,)),
            pltpu.SemaphoreType.DMA((2,)),
            pltpu.SemaphoreType.DMA((2, 3)),
            pltpu.SemaphoreType.DMA((2, 3)),
            pltpu.SemaphoreType.DMA((PIECES - 1,)),
            pltpu.SemaphoreType.DMA((PIECES - 1,)),
        ],
        compiler_params=pltpu.CompilerParams(
            collective_id=0, has_side_effects=True, vmem_limit_bytes=60 * 1024 * 1024
        ),
    )(contrasts, flips)
    inside = mask.astype(f32)
    return high * inside, exceed * inside


def solution(mesh):
    in_specs = (P("subj", "vox", None), P(None, "subj"), P("vox", None))
    out_specs = (P("vox", None), P("vox", None))
    return jax.shard_map(
        per_device, mesh=mesh, in_specs=in_specs, out_specs=out_specs, check_vma=False
    )
```

```python
import functools
import math

import jax
import jax.numpy as jnp
from jax import lax
from jax.experimental import pallas as pl
from jax.experimental.pallas import tpu as pltpu
from jax.sharding import PartitionSpec as P

NX = 91
PY = 109
PLANE = NX * PY
NZ = 64
NF = 48
SUBJ = 1792
RADIUS = 2
EPSILON = 1e-06

TILE = 128
PIECES = 16
CHUNKS = 5
SPAN = TILE * PIECES
WIDE = SPAN * CHUNKS
LANES = TILE * CHUNKS
ROWS = ((24, 24), (24, 24), (24, 24), (24, 24), (24, 24))
PARTS = [(c, sum(rows[:i]), rows[i]) for c, rows in enumerate(ROWS) for i in range(len(rows))]
ITEMS = len(PARTS)
EXTRA = ITEMS
BLOCK = 256
MARGIN = 256
SEG = 1280
AHEAD = 2
NEXT = 1
READY = 2
LAG = 3
ENTRY = 5
ORDER = (*range(ENTRY), EXTRA, *range(ENTRY, ITEMS))

WEIGHT = {k: math.exp(-0.5 * k * k) for k in range(-RADIUS, RADIUS + 1)}
MESH = pl.DeviceIdType.MESH


def row_of(position):
    return (position * 38480) >> 22


def first_bit(i):
    return ((i + 1) // 2) % 2


def second_bit(i):
    return i // 2


def partner(i, kind):
    odd = i % 2
    return (i + 1 - 2 * odd) if kind == 0 else (i + 3 + 2 * odd) % 4


def piece_of(p, y, z):
    bits = (first_bit, second_bit) if p == 0 else (second_bit, first_bit)
    return 8 * bits[0](y) + 4 * bits[1](y) + 2 * bits[0](z) + bits[1](z)


OWNER = [{piece_of(p, d // 4, d % 4): d for d in range(PIECES)} for p in range(2)]


def kernel(
    x_hbm, flips_ref, high_ref, exceed_ref,
    x, w, full, extra, r1, r2, r3, r4, e1, e2, e3, e4, s2, s3, s4, t2, t3, t4,
    square, swept, smooth, before, after, gathered,
    in_sem, send_sem, recv_sem, halo_send, halo_recv, gather_send, gather_recv,
    flat_send, flat_recv,
):
    subj = lax.axis_index("subj")
    vox = lax.axis_index("vox")
    n_vox = lax.axis_size("vox")
    y, z = subj // 4, subj % 4
    up = (vox + 1) % n_vox
    down = (vox + n_vox - 1) % n_vox

    def y_peer(kind):
        return {"subj": partner(y, kind) * 4 + z}

    def z_peer(kind):
        return {"subj": y * 4 + partner(z, kind)}

    loads = []
    for c in range(CHUNKS):
        width = min(SPAN, PLANE - SPAN * c)
        view = (slice(None), slice(None), pl.ds(SPAN * c, width))
        load = pltpu.make_async_copy(x_hbm.at[view], x.at[view], in_sem.at[c])
        load.start()
        loads.append(load)

    barrier = pltpu.get_barrier_semaphore()
    for kind in range(2):
        pl.semaphore_signal(barrier, 1, device_id=y_peer(kind), device_id_type=MESH)
        pl.semaphore_signal(barrier, 1, device_id=z_peer(kind), device_id_type=MESH)
    for other in (up, down):
        pl.semaphore_signal(barrier, 1, device_id={"vox": other}, device_id_type=MESH)

    signs = flips_ref[...].astype(jnp.float32).astype(jnp.bfloat16)
    n_local = signs.shape[1]
    column = lax.broadcasted_iota(jnp.int32, (n_local, 2 * n_local), 1)
    subject = lax.broadcasted_iota(jnp.int32, (n_local, 2 * n_local), 0)
    for p in range(2):
        spread = (column == 2 * subject + p).astype(jnp.float32).astype(jnp.bfloat16)
        w[pl.ds(NF * p, NF), :] = jnp.dot(
            signs, spread, preferred_element_type=jnp.float32
        ).astype(jnp.bfloat16)
    lane = lax.broadcasted_iota(jnp.int32, (16, 2 * n_local), 1)
    line = lax.broadcasted_iota(jnp.int32, (16, 2 * n_local), 0)
    w[pl.ds(2 * NF, 16), :] = (lane % 2 == line).astype(jnp.float32).astype(jnp.bfloat16)

    def multiply(c):
        loads[c].wait()
        for start in range(SPAN * c, min(SPAN * (c + 1), PLANE), BLOCK):
            width = min(BLOCK, PLANE - start)
            values = x[:, :, pl.ds(start, width)].reshape(2 * n_local, width)
            sums = jnp.dot(w[...], values, preferred_element_type=jnp.float32)
            wide = values.astype(jnp.float32)
            squared = jnp.sum((wide * wide).reshape(n_local // 4, 8, width), axis=0)
            second = squared[0:2] + squared[2:4] + squared[4:6] + squared[6:8]
            square[:, pl.ds(MARGIN + start, width)] = second
            for low in range(0, width, TILE):
                size = min(TILE, width - low)
                piece = (start + low) // TILE - PIECES * c
                for p in range(2):
                    row = NF * p
                    full[p, c, piece, :, pl.ds(0, size)] = sums[row:row + NF, low:low + size]
                    row = 2 * NF + p
                    extra[p, piece, pl.ds(0, 1), pl.ds(TILE * c, size)] = sums[row:row + 1, low:low + size]

    keep = []
    for p in range(2):
        bits = (first_bit, second_bit) if p == 0 else (second_bit, first_bit)
        keep.append([bits[0](y), bits[1](y), bits[0](z), bits[1](z)])

    def views(p, item):
        if item == EXTRA:
            return [ref.at[p] for ref in (extra, e1, e2, e3, e4, t2, t3, t4)]
        c, row, rows = PARTS[item]
        at = (p, c, slice(None), pl.ds(row, rows))
        return [ref.at[at] for ref in (full, r1, r2, r3, r4, s2, s3, s4)]

    def send_of(step, p, item):
        held = views(p, item)
        source = [held[0].at[pl.ds(8 * (1 - keep[p][0]), 8)], held[5], held[6], held[7]][step]
        peer = [y_peer(p), y_peer(1 - p), z_peer(p), z_peer(1 - p)][step]
        return pltpu.make_async_remote_copy(
            src_ref=source, dst_ref=held[1 + step],
            send_sem=send_sem.at[step, p, item], recv_sem=recv_sem.at[step, p, item],
            device_id=peer, device_id_type=MESH,
        )

    started = {}

    def start(step, p, item):
        copy = send_of(step, p, item)
        copy.start()
        started[step, p, item] = copy

    def advance(step, item):
        for p in range(2):
            k1, k2, k3, k4 = keep[p]
            started[step, p, item].wait_recv()
            a, b1, b2, b3, _, o2, o3, o4 = views(p, item)
            if step == 0:
                for i in range(4):
                    at = 4 * (1 - k2) + i
                    o2[i] = a[8 * k1 + at] + b1[at]
            elif step == 1:
                for i in range(2):
                    at = 2 * (1 - k3) + i
                    o3[i] = a[8 * k1 + 4 * k2 + at] + b1[4 * k2 + at] + b2[at]
            else:
                at = 1 - k4
                o4[0] = a[8 * k1 + 4 * k2 + 2 * k3 + at] + b1[4 * k2 + 2 * k3 + at] + b2[2 * k3 + at] + b3[at]
            start(step + 1, p, item)

    def total(p, item):
        k1, k2, k3, k4 = keep[p]
        started[3, p, item].wait_recv()
        a, b1, b2, b3, b4 = views(p, item)[:5]
        return a[8 * k1 + 4 * k2 + 2 * k3 + k4] + b1[4 * k2 + 2 * k3 + k4] + b2[2 * k3 + k4] + b3[k4] + b4[0]

    def shifted(ref, base, offset):
        padded = ref[:, pl.ds(base, SEG + 2 * MARGIN)]
        return pltpu.roll(padded, (-offset) % (SEG + 2 * MARGIN), 1)[:, MARGIN:MARGIN + SEG]

    def in_plane():
        @pl.loop(0, WIDE // SEG)
        def _(i):
            base = pl.multiple_of(i * SEG, TILE)
            position = base + lax.broadcasted_iota(jnp.int32, (2, SEG), 1)
            at = position - PY * row_of(position)
            result = jnp.zeros((2, SEG), jnp.float32)
            for k in range(-RADIUS, RADIUS + 1):
                moved = shifted(square, base, k)
                inside = (at + k >= 0) & (at + k < PY)
                result = result + WEIGHT[k] * jnp.where(inside, moved, 0.0)
            swept[:, pl.ds(pl.multiple_of(base + MARGIN, TILE), SEG)] = result

        @pl.loop(0, WIDE // SEG)
        def _(i):
            base = pl.multiple_of(i * SEG, TILE)
            result = jnp.zeros((2, SEG), jnp.float32)
            for k in range(-RADIUS, RADIUS + 1):
                result = result + WEIGHT[k] * shifted(swept, base, k * PY)
            smooth[:, pl.ds(base, SEG)] = result

    halo = [
        pltpu.make_async_remote_copy(
            src_ref=smooth, dst_ref=target, send_sem=halo_send.at[i], recv_sem=halo_recv.at[i],
            device_id={"vox": other}, device_id_type=MESH,
        )
        for i, (target, other) in enumerate(((before, up), (after, down)))
    ]

    def depth():
        for copy in halo:
            copy.wait_recv()
        first = vox > 0
        last = vox < n_vox - 1
        for i in range(0, WIDE, SEG):
            place = pl.ds(i, SEG)
            lower = jnp.where(first, before[:, place], 0.0)
            upper = jnp.where(last, after[:, place], 0.0)
            own = smooth[:, place]
            rows = (
                WEIGHT[2] * lower[0:1] + WEIGHT[1] * lower[1:2] + own[0:1] + WEIGHT[1] * own[1:2] + WEIGHT[2] * upper[0:1],
                WEIGHT[2] * lower[1:2] + WEIGHT[1] * own[0:1] + own[1:2] + WEIGHT[1] * upper[0:1] + WEIGHT[2] * upper[1:2],
            )
            for low in range(0, SEG, TILE):
                tile = (i + low) // TILE
                for p in range(2):
                    extra[p, tile % PIECES, pl.ds(1, 1), pl.ds(TILE * (tile // PIECES), TILE)] = rows[p][:, low:low + TILE]

    for c in range(READY):
        multiply(c)
    pl.semaphore_wait(barrier, 6)
    for item in ORDER[:AHEAD]:
        for p in range(2):
            start(0, p, item)

    zeros = jnp.zeros((2, MARGIN), jnp.float32)
    square[:, pl.ds(0, MARGIN)] = zeros
    edge = PLANE // TILE * TILE
    square[:, pl.ds(MARGIN + edge, WIDE + MARGIN - edge)] = jnp.zeros((2, WIDE + MARGIN - edge), jnp.float32)
    swept[:, pl.ds(0, MARGIN)] = zeros
    swept[:, pl.ds(MARGIN + WIDE, MARGIN)] = zeros
    for p in range(2):
        for i in range(edge // TILE % PIECES, PIECES):
            full[p, CHUNKS - 1, i] = jnp.zeros((NF, TILE), jnp.float32)
            extra[p, i, pl.ds(0, 1), pl.ds(LANES - TILE, TILE)] = jnp.zeros((1, TILE), jnp.float32)
    for c in range(READY, CHUNKS):
        multiply(c)
    in_plane()
    for copy in halo:
        copy.start()

    n = len(ORDER)
    for t in range(n + LAG):
        if t < n:
            advance(0, ORDER[t])
            if t + AHEAD < n:
                if ORDER[t + AHEAD] == EXTRA:
                    depth()
                for p in range(2):
                    start(0, p, ORDER[t + AHEAD])
        if 0 <= t - NEXT < n:
            advance(1, ORDER[t - NEXT])
        if 0 <= t - LAG < n:
            advance(2, ORDER[t - LAG])

    number = jnp.float32(SUBJ)
    scales = []
    for p in range(2):
        k1, k2, k3, k4 = keep[p]
        piece = 8 * k1 + 4 * k2 + 2 * k3 + k4
        spot = lax.broadcasted_iota(jnp.int32, (1, LANES), 1)
        position = (PIECES * (spot >> 7) + piece) * TILE + (spot & 127)
        at_x = row_of(position)
        at_y = position - PY * at_x
        level = 2 * vox + p + jnp.zeros((1, LANES), jnp.int32)
        norms = []
        for at, size in ((at_x, NX), (at_y, PY), (level, NZ)):
            norm = jnp.zeros((1, LANES), jnp.float32)
            for k in range(-RADIUS, RADIUS + 1):
                norm = norm + jnp.where((at + k >= 0) & (at + k < size), jnp.float32(WEIGHT[k]), 0.0)
            norms.append(norm)
        sums = total(p, EXTRA)
        sigma = jnp.sqrt(sums[1:2] / number / (norms[0] * norms[1] * norms[2]) + EPSILON)
        denominator = jnp.sqrt(number) * sigma
        scales.append((denominator, sums[0:1] / denominator))

    def finish(c):
        place = slice(TILE * c, TILE * (c + 1))
        for p in range(2):
            denominator, observed = (scale[:, place] for scale in scales[p])
            best = jnp.full((8, TILE), -1e30, jnp.float32)
            share = jnp.zeros((8, TILE), jnp.float32)
            for item, part in enumerate(PARTS):
                if part[0] == c:
                    tflip = total(p, item) / denominator
                    chance = jax.nn.sigmoid(2.0 * (tflip - observed))
                    for low in range(0, part[2], 8):
                        best = jnp.maximum(best, tflip[low:low + 8])
                        share = share + chance[low:low + 8]
            gathered[subj, c, pl.ds(2 * p, 1), :] = jnp.max(best, axis=0, keepdims=True)
            gathered[subj, c, pl.ds(2 * p + 1, 1), :] = jnp.sum(share, axis=0, keepdims=True) / NF

    returned = []

    def give(place, peers, send, recv):
        copies = []
        for d, peer in peers:
            copy = pltpu.make_async_remote_copy(
                src_ref=place, dst_ref=place, send_sem=send.at[d - 1], recv_sem=recv.at[d - 1],
                device_id={"subj": peer}, device_id_type=MESH,
            )
            copy.start()
            copies.append(copy)
        returned.extend(copies)
        return copies

    z_peers = [(d, y * 4 + (z + d) % 4) for d in (2, 1, 3)]
    y_peers = [(d, (y + d) % 4 * 4 + z) for d in (2, 1, 3)]
    early, late = pl.ds(0, CHUNKS - 1), pl.ds(CHUNKS - 1, 1)

    def arrived(copies):
        for copy in copies:
            copy.wait_recv()

    def write(chunks):
        for c in chunks:
            for i in range(PIECES):
                begin = SPAN * c + TILE * i
                width = min(TILE, PLANE - begin)
                if width <= 0:
                    continue
                for p in range(2):
                    for kind, ref in enumerate((high_ref, exceed_ref)):
                        ref[pl.ds(p, 1), pl.ds(begin, width)] = gathered[OWNER[p][i], c, pl.ds(2 * p + kind, 1), pl.ds(0, width)]

    for c in range(CHUNKS - 1):
        finish(c)
    z_early = give(gathered.at[pl.ds(subj, 1), early], z_peers, gather_send.at[0], gather_recv.at[0])
    finish(CHUNKS - 1)
    all_peers = [
        (4 * e + d, (y + e) % 4 * 4 + (z + d) % 4) for d in (2, 1, 3, 0) for e in (2, 1, 3, 0) if d or e
    ]
    flat = give(gathered.at[pl.ds(subj, 1), late], all_peers, flat_send, flat_recv)
    arrived(z_early)
    y_early = give(gathered.at[pl.ds(4 * y, 4), early], y_peers, gather_send.at[1], gather_recv.at[1])
    arrived(y_early)
    write(range(CHUNKS - 1))
    arrived(flat)
    write((CHUNKS - 1,))

    for copy in list(started.values()) + halo + returned:
        copy.wait_send()


def per_device(contrasts, flips, mask):
    local, depth, cells = contrasts.shape
    f32 = jnp.float32
    vmem = pltpu.VMEM
    high, exceed = pl.pallas_call(
        kernel,
        out_shape=[jax.ShapeDtypeStruct((depth, cells), f32)] * 2,
        in_specs=[pl.BlockSpec(memory_space=pl.ANY), pl.BlockSpec(memory_space=vmem)],
        out_specs=[pl.BlockSpec(memory_space=vmem)] * 2,
        scratch_shapes=[
            vmem((local, 2, cells), jnp.bfloat16),
            vmem((2 * NF + 16, 2 * local), jnp.bfloat16),
            vmem((2, CHUNKS, PIECES, NF, TILE), f32),
            vmem((2, PIECES, 2, LANES), f32),
            *[vmem((2, CHUNKS, m, NF, TILE), f32) for m in (8, 4, 2, 1)],
            *[vmem((2, m, 2, LANES), f32) for m in (8, 4, 2, 1)],
            *[vmem((2, CHUNKS, m, NF, TILE), f32) for m in (4, 2, 1)],
            *[vmem((2, m, 2, LANES), f32) for m in (4, 2, 1)],
            vmem((2, WIDE + 2 * MARGIN), f32),
            vmem((2, WIDE + 2 * MARGIN), f32),
            vmem((2, WIDE), f32),
            vmem((2, WIDE), f32),
            vmem((2, WIDE), f32),
            vmem((PIECES, CHUNKS, 4, TILE), f32),
            pltpu.SemaphoreType.DMA((CHUNKS,)),
            pltpu.SemaphoreType.DMA((4, 2, ITEMS + 1)),
            pltpu.SemaphoreType.DMA((4, 2, ITEMS + 1)),
            pltpu.SemaphoreType.DMA((2,)),
            pltpu.SemaphoreType.DMA((2,)),
            pltpu.SemaphoreType.DMA((2, 3)),
            pltpu.SemaphoreType.DMA((2, 3)),
            pltpu.SemaphoreType.DMA((PIECES - 1,)),
            pltpu.SemaphoreType.DMA((PIECES - 1,)),
        ],
        compiler_params=pltpu.CompilerParams(
            collective_id=0, has_side_effects=True, vmem_limit_bytes=60 * 1024 * 1024
        ),
    )(contrasts, flips)
    inside = mask.astype(f32)
    return high * inside, exceed * inside


def solution(mesh):
    in_specs = (P("subj", "vox", None), P(None, "subj"), P("vox", None))
    out_specs = (P("vox", None), P("vox", None))
    return jax.shard_map(
        per_device, mesh=mesh, in_specs=in_specs, out_specs=out_specs, check_vma=False
    )
```
